32 devices in a mesh: blk: 8 (over y, x, core), slab: 4 (over z).
Axes of the slice: x: 2, y: 2, z: 4, core: 2. Of those that a mesh axis runs over, the one named last changes fastest.
Arguments:
- old_factor: bfloat16 [8192, 24576], P('slab', 'blk'), may hold values from -0.0546875 to 0.0546875
- solved: bfloat16 [24576, 256], P('blk', 'slab'), may hold values from -6 to 6
- band: bfloat16 [8192, 8192], P('blk'), may hold values from -0.0625 to 0.0625
- inv_diag: bfloat16 [2048, 8192], P(None, 'blk'), may hold values from -1 to 2, as said below
- rhs: bfloat16 [8192, 256], P('blk', 'slab'), may hold values from -6 to 6
Outputs:
- solution: bfloat16 [8192, 256], P('blk', 'slab')
The draws below stay inside these ranges and needn't reach their ends.
Inputs may be any that keep to these rules, and one draw needn't show every extreme that they name: `inv_diag`: columns k * 2048 to (k + 1) * 2048 - 1 hold the inverse applied in block step k.
All inputs are finite; a program needn't handle non-finite values.
Results may differ from the reference program's by a relative error of at most 0.008.
Values may be sent and summed in bfloat16 or wider, within the bound.
A program may use at most 64 MiB of HBM per device.

```python
import math
import jax
import jax.numpy as jnp
from jax import lax

NB = 2048
STEPS = 4
W = 8192
N_OLD = 24576
S = 256


def draw_inv_diag(key, part):
    row_pos = jnp.arange(NB)[:, None]
    col_pos = jnp.arange(W)[None, :] % NB
    unit = (row_pos == col_pos).astype(jnp.float32)
    first, second = jax.random.split(key)
    noise = jnp.clip(jax.random.normal(first, (NB, W), jnp.float32), -3.0, 3.0) * 0.5 / math.sqrt(NB)
    scales = jax.random.uniform(second, (1, W), jnp.float32, 0.8, 1.2)
    return (unit * scales + noise).astype(jnp.bfloat16)


def strengthened(array, key, source, target, parts, factor):
    def block_of(dim):
        return (jnp.arange(array.shape[dim]) // (array.shape[dim] // parts)).reshape((-1,) + (1,) * (array.ndim - 1 - dim))

    first = jax.random.permutation(key, parts)[block_of(target)]
    far = (block_of(target) + parts // 2) % parts
    return jnp.where((block_of(source) == first) | (block_of(source) == far), factor * array, array)


def level_of(rng, dims, cuts, low, top_value):
    def one(position, blocks):
        heights = jax.random.uniform(jax.random.fold_in(jax.random.fold_in(rng, 6), position), (blocks,), jnp.float32, low / len(cuts), top_value / len(cuts))
        return jnp.repeat(jnp.exp(heights), dims[position] // blocks).reshape((-1,) + (1,) * (len(dims) - position - 1))

    level = one(*cuts[0])
    for cut in cuts[1:]:
        level = level * one(*cut)
    return level


def bell_draw(own_key, shape, deviation, most, pieces=(), kind=jnp.bfloat16):
    array = jax.random.normal(own_key, shape, jnp.float32) * deviation
    if len(pieces) > 0:
        array = level_of(own_key, shape, pieces, -0.22, 0.18) * array
    return jnp.clip(array, min=-most, max=most).astype(kind)


def noise_with(rng, extent, scale, most, pieces, heavy, held_as=jnp.bfloat16):
    drawn = scale * jax.random.normal(rng, extent, jnp.float32)
    if pieces:
        drawn = drawn * level_of(rng, extent, pieces, -0.22, 0.18)
    return jnp.clip(strengthened(drawn, jax.random.fold_in(rng, 3), *heavy), -most, most).astype(held_as)


def setup_inputs(seed: int = 0) -> dict:
    splits = jax.random.split(jax.random.key(seed), 6)
    return {
        "old_factor": noise_with(splits[0], (W, N_OLD), N_OLD ** -0.5, 0.0546875, ((0, 4), (1, 8)), (1, 0, 8, 2.0)),
        "solved": bell_draw(splits[1], (N_OLD, S), 1.0, 6.0, ((0, 8), (1, 4))),
        "band": bell_draw(splits[2], (W, W), W ** -0.5, 0.0625, ((0, 8),)),
        "inv_diag": draw_inv_diag(jax.random.fold_in(splits[5], 71), 0),
        "rhs": bell_draw(splits[4], (W, S), 1.0, 6.0, ((0, 8), (1, 4))),
    }


def reference(old_factor, solved, band, inv_diag, rhs):
    earlier = jnp.dot(old_factor, solved, preferred_element_type=jnp.float32)
    solution = jnp.zeros((W, S), jnp.bfloat16)
    for index in range(STEPS):
        start = index * NB
        rows = band[start:start + NB, :]
        carried = jnp.dot(rows, solution, preferred_element_type=jnp.float32)
        source = rhs[start:start + NB, :].astype(jnp.float32)
        before = earlier[start:start + NB, :]
        resid = (source - before - carried).astype(jnp.bfloat16)
        inverse = inv_diag[:, start:start + NB]
        block = jnp.dot(inverse, resid, preferred_element_type=jnp.float32).astype(jnp.bfloat16)
        solution = lax.dynamic_update_slice_in_dim(solution, block, start, 0)
    return solution
```

```python
import functools

import jax
import jax.numpy as jnp
from jax import lax
from jax.experimental import pallas as pl
from jax.experimental.pallas import tpu as pltpu
from jax.sharding import PartitionSpec as P

STEPS = 4
CHUNKS = 2
MESH = pl.DeviceIdType.MESH
F32 = jnp.float32
BF16 = jnp.bfloat16


def swap_halves(value):
    return pltpu.roll(value, value.shape[1] // 2, 1)


def left_half(shape):
    return lax.broadcasted_iota(jnp.int32, shape, 1) < shape[1] // 2


def pack(upper, lower):
    return jnp.where(left_half(upper.shape), upper, swap_halves(lower))


def product(matrix_ref, rows, packed):
    half = packed.shape[0]
    first = jnp.dot(matrix_ref[rows, :half], packed, preferred_element_type=F32)
    second = jnp.dot(matrix_ref[rows, half:], packed, preferred_element_type=F32)
    return first + swap_halves(second)


def kernel(
    n_blk,
    n_slab,
    factor_hbm,
    solved_ref,
    band_hbm,
    inv_hbm,
    rhs_ref,
    out_ref,
    factor,
    band,
    inv,
    shards,
    parts,
    arrived,
    reduced,
    earlier,
    accum,
    resid,
    newest,
    factor_sem,
    band_sem,
    inv_sem,
    inv_send,
    shard_recv,
    up_send,
    down_send,
    part_send,
    part_recv,
    red_send,
    red_recv,
    resid_send,
    resid_recv,
    new_send,
    new_recv,
    fwd_send,
):
    b = lax.axis_index("blk")
    s = lax.axis_index("slab")
    width = rhs_ref.shape[1]
    own_rows = rhs_ref.shape[0]
    block_rows = inv_hbm.shape[0]
    group = block_rows // own_rows
    own_block = b // group
    member = b % group
    window = factor_hbm.shape[0]
    piece = shards.shape[1] // CHUNKS
    half = parts.shape[2]
    per_owner = own_rows // (2 * half)
    owners = window // own_rows
    tiles = factor_sem.shape[0]
    tile = window // tiles

    def remote(src, dst, send, recv, blk, slab):
        return pltpu.make_async_remote_copy(
            src_ref=src, dst_ref=dst, send_sem=send, recv_sem=recv,
            device_id=(blk, slab), device_id_type=MESH,
        )

    depth = solved_ref.shape[0]
    upper = solved_ref[: depth // 2, :].astype(F32)
    lower = solved_ref[depth // 2 :, :].astype(F32)
    shards[s] = jnp.concatenate([upper, lower], axis=1).astype(BF16)

    def shard_copy(which, chunk, up):
        ref = shards.at[which, pl.ds(chunk * piece, piece)]
        send = up_send if up else down_send
        return remote(ref, ref, send.at[which, chunk], shard_recv.at[which, chunk], b, s + 1 if up else s - 1)

    def pass_on(which, chunk, up):
        @pl.when(s < n_slab - 1 if up else s > 0)
        def _():
            shard_copy(which, chunk, up).start()

    for chunk in range(CHUNKS):
        pass_on(s, chunk, True)
        pass_on(s, chunk, False)

    def factor_copy(t):
        rows = pl.ds(t * tile, tile)
        return pltpu.make_async_copy(factor_hbm.at[rows], factor.at[rows], factor_sem.at[t])

    for t in range(tiles):
        factor_copy(t).start()

    def inv_remote(peer):
        return remote(
            inv_hbm.at[pl.ds(peer * own_rows, own_rows)], inv.at[member],
            inv_send.at[peer], inv_sem.at[member], own_block * group + peer, s,
        )

    inv_own = pltpu.make_async_copy(
        inv_hbm.at[pl.ds(member * own_rows, own_rows)], inv.at[member], inv_sem.at[member]
    )
    inv_own.start()
    for d in range(1, group):
        inv_remote((member + d) % group).start()

    def band_copy(k, m):
        return pltpu.make_async_copy(
            band_hbm.at[:, pl.ds(k * block_rows + m * own_rows, own_rows)], band.at[k, m], band_sem.at[k, m]
        )

    for k in range(STEPS - 1):
        @pl.when(own_block > k)
        def _():
            for m in range(group):
                band_copy(k, m).start()

    def part_copy(which, d):
        c = (b + d) % n_blk
        return remote(
            parts.at[which, c], arrived.at[which, n_blk - d - 1],
            part_send.at[which], part_recv.at[which], c, s,
        )

    def multiply(which, first_time):
        def step(t, carry):
            if first_time:
                factor_copy(t).wait()
            rows = pl.ds(t * tile, tile)
            value = product(factor, rows, shards[which])
            for i in range(tile // (2 * half)):
                base = i * 2 * half
                packed = pack(value[base : base + half], value[base + half : base + 2 * half])
                parts[which, t * (tile // (2 * half)) + i] = packed.astype(BF16)
            return carry

        lax.fori_loop(0, tiles, step, 0)
        lax.fori_loop(1, n_blk, lambda d, carry: (part_copy(which, d).start(), carry)[1], 0)

    def red_remote(which):
        return remote(
            reduced.at[which], earlier.at[b % per_owner],
            red_send.at[which], red_recv.at[b % per_owner], s * owners + b // per_owner, which,
        )

    def red_local(which):
        return pltpu.make_async_copy(reduced.at[which], earlier.at[b % per_owner], red_recv.at[b % per_owner])

    def is_self(which):
        return jnp.logical_and(which == s, b == s * owners + b // per_owner)

    def all_parts(which):
        return pltpu.make_async_copy(arrived.at[which], arrived.at[which], part_recv.at[which])

    def combine(which):
        all_parts(which).wait()
        total = parts[which, b].astype(F32)
        for d in range(n_blk - 1):
            total = total + arrived[which, d].astype(F32)
        reduced[which] = total

        @pl.when(is_self(which))
        def _():
            red_local(which).start()

        @pl.when(jnp.logical_not(is_self(which)))
        def _():
            red_remote(which).start()

    def take(which, up):
        for chunk in range(CHUNKS):
            ref = shards.at[which, pl.ds(chunk * piece, piece)]
            remote(ref, ref, up_send.at[which, chunk], shard_recv.at[which, chunk], b, s).wait_recv()
            pass_on(which, chunk, up)

    def at_distance(t, action):
        if t == 0:
            action(s, None)
            return

        @pl.when(s >= t)
        def _():
            action(s - t, True)

        @pl.when(s + t < n_slab)
        def _():
            action(s + t, False)

    multiply(s, True)
    for t in range(1, n_slab):
        at_distance(t, take)
        at_distance(t, lambda which, up: multiply(which, False))
        at_distance(t - 1, lambda which, up: combine(which))
    at_distance(n_slab - 1, lambda which, up: combine(which))

    accum[:, :width] = rhs_ref[...].astype(F32)
    for i in range(per_owner):
        pltpu.make_async_copy(reduced.at[0], earlier.at[i], red_recv.at[i]).wait()
        base = i * 2 * half
        value = earlier[i]
        accum[base : base + half, :width] = accum[base : base + half, :width] - value[:, :width]
        low = swap_halves(value)
        accum[base + half : base + 2 * half, :width] = accum[base + half : base + 2 * half, :width] - low[:, :width]

    top = own_rows // 2
    row_tiles = max(1, own_rows // 256)
    row_tile = own_rows // row_tiles

    def resid_copy(peer):
        ref = resid.at[member]
        return remote(ref, ref, resid_send.at[peer], resid_recv.at[member], own_block * group + peer, s)

    def new_copy(k, j):
        ref = newest.at[k, member]
        return remote(ref, ref, new_send.at[k, j], new_recv.at[k, member], j * group + member, s)

    def forward_copy(k, peer):
        ref = newest.at[k, member]
        return remote(ref, ref, fwd_send.at[k, peer], new_recv.at[k, member], own_block * group + peer, s)

    def add_product(matrix_ref, packed, sign, fresh):
        def step(t, carry):
            rows = pl.ds(t * row_tile, row_tile)
            value = product(matrix_ref, rows, packed)
            if fresh:
                accum[rows, :] = value
            else:
                accum[rows, :] = accum[rows, :] + sign * value
            return carry

        lax.fori_loop(0, row_tiles, step, 0)

    for k in range(STEPS):
        @pl.when(own_block == k)
        def _():
            resid[member] = pack(accum[:top, :], accum[top:, :]).astype(BF16)
            for d in range(1, group):
                resid_copy((member + d) % group).start()
            inv_own.wait()
            add_product(inv.at[member], resid[member], 1.0, True)
            for d in range(1, group):
                peer = (member + d) % group
                pltpu.make_async_copy(inv_hbm.at[pl.ds(0, own_rows)], inv.at[peer], inv_sem.at[peer]).wait()
                pltpu.make_async_copy(resid.at[peer], resid.at[peer], resid_recv.at[peer]).wait()
                add_product(inv.at[peer], resid[peer], 1.0, False)
            if k + 1 < STEPS:
                newest[k, member] = pack(accum[:top, :], accum[top:, :]).astype(BF16)
                for j in range(k + 1, STEPS):
                    new_copy(k, j).start()
            out_ref[...] = accum[:, :width].astype(BF16)

        if k + 1 < STEPS:
            @pl.when(own_block > k)
            def _():
                ref = newest.at[k, member]
                pltpu.make_async_copy(ref, ref, new_recv.at[k, member]).wait()
                for d in range(1, group):
                    forward_copy(k, (member + d) % group).start()
                for m in range(group):
                    band_copy(k, m).wait()
                add_product(band.at[k, member], newest[k, member], -1.0, False)
                for d in range(1, group):
                    peer = (member + d) % group
                    ref = newest.at[k, peer]
                    pltpu.make_async_copy(ref, ref, new_recv.at[k, peer]).wait()
                    add_product(band.at[k, peer], newest[k, peer], -1.0, False)

    def sent(which, up):
        for chunk in range(CHUNKS):
            for way in (True, False):
                if up is None or up == way:
                    @pl.when(s < n_slab - 1 if way else s > 0)
                    def _():
                        shard_copy(which, chunk, way).wait_send()
        pltpu.make_async_copy(arrived.at[which], arrived.at[which], part_send.at[which]).wait()

        @pl.when(jnp.logical_not(is_self(which)))
        def _():
            red_remote(which).wait_send()

    for t in range(n_slab):
        at_distance(t, sent)
    for d in range(1, group):
        peer = (member + d) % group
        inv_remote(peer).wait_send()
        resid_copy(peer).wait_send()
    for k in range(STEPS - 1):
        @pl.when(own_block == k)
        def _():
            for j in range(k + 1, STEPS):
                new_copy(k, j).wait_send()

        @pl.when(own_block > k)
        def _():
            for d in range(1, group):
                forward_copy(k, (member + d) % group).wait_send()


def body(n_blk, n_slab, old_factor, solved, band, inv_diag, rhs):
    window, depth = old_factor.shape
    own_rows, width = rhs.shape
    block_rows = inv_diag.shape[0]
    group = block_rows // own_rows
    half = window // n_blk // 2
    per_owner = own_rows // (2 * half)
    lanes = 2 * width
    tiles = 4
    dma = pltpu.SemaphoreType.DMA
    vmem = pl.BlockSpec(memory_space=pltpu.VMEM)
    hbm = pl.BlockSpec(memory_space=pl.ANY)
    return pl.pallas_call(
        functools.partial(kernel, n_blk, n_slab),
        out_shape=jax.ShapeDtypeStruct(rhs.shape, BF16),
        in_specs=[hbm, vmem, hbm, hbm, vmem],
        out_specs=vmem,
        scratch_shapes=[
            pltpu.VMEM((window, depth), BF16),
            pltpu.VMEM((STEPS - 1, group, own_rows, own_rows), BF16),
            pltpu.VMEM((group, own_rows, own_rows), BF16),
            pltpu.VMEM((n_slab, depth // 2, lanes), BF16),
            pltpu.VMEM((n_slab, n_blk, half, lanes), BF16),
            pltpu.VMEM((n_slab, n_blk - 1, half, lanes), BF16),
            pltpu.VMEM((n_slab, half, lanes), F32),
            pltpu.VMEM((per_owner, half, lanes), F32),
            pltpu.VMEM((own_rows, lanes), F32),
            pltpu.VMEM((group, own_rows // 2, lanes), BF16),
            pltpu.VMEM((STEPS - 1, group, own_rows // 2, lanes), BF16),
            dma((tiles,)),
            dma((STEPS - 1, group)),
            dma((group,)),
            dma((group,)),
            dma((n_slab, CHUNKS)),
            dma((n_slab, CHUNKS)),
            dma((n_slab, CHUNKS)),
            dma((n_slab,)),
            dma((n_slab,)),
            dma((n_slab,)),
            dma((per_owner,)),
            dma((group,)),
            dma((group,)),
            dma((STEPS - 1, STEPS)),
            dma((STEPS - 1, group)),
            dma((STEPS - 1, group)),
        ],
        compiler_params=pltpu.CompilerParams(has_side_effects=True, vmem_limit_bytes=60 * 1024 * 1024),
        name="forward_window",
    )(old_factor, solved, band, inv_diag, rhs)


def solution(mesh):
    return jax.shard_map(
        functools.partial(body, mesh.shape["blk"], mesh.shape["slab"]),
        mesh=mesh,
        in_specs=(
            P("slab", "blk"),
            P("blk", "slab"),
            P("blk", None),
            P(None, "blk"),
            P("blk", "slab"),
        ),
        out_specs=P("blk", "slab"),
        check_vma=False,
    )
```

```python
import functools

import jax
import jax.numpy as jnp
from jax import lax
from jax.experimental import pallas as pl
from jax.experimental.pallas import tpu as pltpu
from jax.sharding import PartitionSpec as P

STEPS = 4
CHUNKS = 2
MESH = pl.DeviceIdType.MESH
F32 = jnp.float32
BF16 = jnp.bfloat16


def swap_halves(value):
    return pltpu.roll(value, value.shape[1] // 2, 1)


def left_half(shape):
    return lax.broadcasted_iota(jnp.int32, shape, 1) < shape[1] // 2


def pack(upper, lower):
    return jnp.where(left_half(upper.shape), upper, swap_halves(lower))


def product(matrix_ref, rows, packed):
    half = packed.shape[0]
    first = jnp.dot(matrix_ref[rows, :half], packed, preferred_element_type=F32)
    second = jnp.dot(matrix_ref[rows, half:], packed, preferred_element_type=F32)
    return first + swap_halves(second)


def kernel(
    n_blk,
    n_slab,
    factor_hbm,
    solved_hbm,
    band_hbm,
    inv_hbm,
    rhs_ref,
    out_ref,
    factor,
    band,
    inv,
    shards,
    columns,
    partial,
    parts,
    arrived,
    reduced,
    earlier,
    accum,
    resid,
    newest,
    factor_sem,
    band_sem,
    inv_sem,
    inv_send,
    shard_recv,
    up_send,
    down_send,
    part_send,
    part_recv,
    red_send,
    red_recv,
    resid_send,
    resid_recv,
    new_send,
    new_recv,
    fwd_send,
):
    b = lax.axis_index("blk")
    s = lax.axis_index("slab")
    width, own_rows = rhs_ref.shape
    block_rows = inv_hbm.shape[0]
    group = block_rows // own_rows
    own_block = b // group
    member = b % group
    window = factor_hbm.shape[0]
    piece = shards.shape[3]
    half = parts.shape[2]
    per_owner = own_rows // (2 * half)
    owners = window // own_rows
    tiles = factor_sem.shape[0]
    tile = window // tiles

    def remote(src, dst, send, recv, blk, slab):
        return pltpu.make_async_remote_copy(
            src_ref=src, dst_ref=dst, send_sem=send, recv_sem=recv,
            device_id=(blk, slab), device_id_type=MESH,
        )

    def shard_copy(which, chunk, up, own):
        ref = shards.at[which, chunk]
        source = solved_hbm.at[:, pl.ds(chunk * piece, piece)] if own else ref
        send = up_send if up else down_send
        return remote(source, ref, send.at[which, chunk], shard_recv.at[which, chunk], b, s + 1 if up else s - 1)

    def pass_on(which, chunk, up, own=False):
        @pl.when(s < n_slab - 1 if up else s > 0)
        def _():
            shard_copy(which, chunk, up, own).start()

    def own_copy(chunk):
        return pltpu.make_async_copy(
            solved_hbm.at[:, pl.ds(chunk * piece, piece)], shards.at[s, chunk], shard_recv.at[s, chunk]
        )

    for chunk in range(CHUNKS):
        pass_on(s, chunk, True, True)
        pass_on(s, chunk, False, True)
        own_copy(chunk).start()

    def factor_copy(t):
        rows = pl.ds(t * tile, tile)
        return pltpu.make_async_copy(factor_hbm.at[rows], factor.at[rows], factor_sem.at[t])

    for t in range(tiles):
        factor_copy(t).start()

    def inv_remote(peer):
        return remote(
            inv_hbm.at[pl.ds(peer * own_rows, own_rows)], inv.at[member],
            inv_send.at[peer], inv_sem.at[member], own_block * group + peer, s,
        )

    inv_own = pltpu.make_async_copy(
        inv_hbm.at[pl.ds(member * own_rows, own_rows)], inv.at[member], inv_sem.at[member]
    )
    inv_own.start()
    for d in range(1, group):
        inv_remote((member + d) % group).start()

    def band_copy(k, m):
        return pltpu.make_async_copy(
            band_hbm.at[:, pl.ds(k * block_rows + m * own_rows, own_rows)], band.at[k, m], band_sem.at[k, m]
        )

    for k in range(STEPS - 1):
        @pl.when(own_block > k)
        def _():
            for m in range(group):
                band_copy(k, m).start()

    def part_copy(which, c):
        return remote(
            parts.at[which, c], arrived.at[which, lax.rem(b - c + n_blk, n_blk) - 1],
            part_send.at[which], part_recv.at[which], c, s,
        )

    def multiply(which, chunk, first_time, side):
        columns[...] = jnp.swapaxes(shards[which, chunk].astype(F32), 0, 1).astype(BF16)
        span = slice(chunk * piece, (chunk + 1) * piece)
        per_tile = tile // (2 * half)

        def step(i, carry):
            t = lax.rem(i + lax.div(b * tiles, n_blk), tiles)
            if first_time and chunk == 0:
                factor_copy(t).wait()
            rows = pl.ds(t * tile, tile)
            value = jnp.dot(factor[rows, span], columns[...], preferred_element_type=F32)
            if chunk > 0:
                value = partial[side, rows, :] + value
            if chunk < CHUNKS - 1:
                partial[side, rows, :] = value
                return carry
            for i in range(per_tile):
                base = i * 2 * half
                c = t * per_tile + i
                packed = jnp.concatenate([value[base : base + half], value[base + half : base + 2 * half]], axis=1)
                parts[which, c] = packed.astype(BF16)

                @pl.when(c != b)
                def _():
                    part_copy(which, c).start()

            return carry

        lax.fori_loop(0, tiles, step, 0)

    def red_remote(which):
        return remote(
            reduced.at[which], earlier.at[b % per_owner],
            red_send.at[which], red_recv.at[b % per_owner], s * owners + b // per_owner, which,
        )

    def red_local(which):
        return pltpu.make_async_copy(reduced.at[which], earlier.at[b % per_owner], red_recv.at[b % per_owner])

    def is_self(which):
        return jnp.logical_and(which == s, b == s * owners + b // per_owner)

    def all_parts(which):
        return pltpu.make_async_copy(arrived.at[which], arrived.at[which], part_recv.at[which])

    def combine(which):
        all_parts(which).wait()
        total = parts[which, b].astype(F32)
        for d in range(n_blk - 1):
            total = total + arrived[which, d].astype(F32)
        reduced[which] = total

        @pl.when(is_self(which))
        def _():
            red_local(which).start()

        @pl.when(jnp.logical_not(is_self(which)))
        def _():
            red_remote(which).start()

    def take(which, chunk, up):
        ref = shards.at[which, chunk]
        remote(ref, ref, up_send.at[which, chunk], shard_recv.at[which, chunk], b, s).wait_recv()
        pass_on(which, chunk, up)

    def at_distance(t, action):
        if t == 0:
            action(s, None)
            return

        @pl.when(s >= t)
        def _():
            action(s - t, True)

        @pl.when(s + t < n_slab)
        def _():
            action(s + t, False)

    for chunk in range(CHUNKS):
        own_copy(chunk).wait()
        multiply(s, chunk, True, 0)
    for t in range(1, n_slab):
        for chunk in range(CHUNKS):
            at_distance(t, lambda which, up: take(which, chunk, up))
            at_distance(t, lambda which, up: multiply(which, chunk, False, 0 if up else 1))
        at_distance(t - 1, lambda which, up: combine(which))
    at_distance(n_slab - 1, lambda which, up: combine(which))

    accum[:, :width] = jnp.swapaxes(rhs_ref[...].astype(F32), 0, 1)
    for i in range(per_owner):
        pltpu.make_async_copy(reduced.at[0], earlier.at[i], red_recv.at[i]).wait()
        base = i * 2 * half
        value = earlier[i]
        accum[base : base + half, :width] = accum[base : base + half, :width] - value[:, :width]
        low = swap_halves(value)
        accum[base + half : base + 2 * half, :width] = accum[base + half : base + 2 * half, :width] - low[:, :width]

    top = own_rows // 2
    row_tiles = max(1, own_rows // 256)
    row_tile = own_rows // row_tiles

    def resid_copy(peer):
        ref = resid.at[member]
        return remote(ref, ref, resid_send.at[peer], resid_recv.at[member], own_block * group + peer, s)

    def new_copy(k, j):
        ref = newest.at[k, member]
        return remote(ref, ref, new_send.at[k, j], new_recv.at[k, member], j * group + member, s)

    def forward_copy(k, peer):
        ref = newest.at[k, member]
        return remote(ref, ref, fwd_send.at[k, peer], new_recv.at[k, member], own_block * group + peer, s)

    def add_product(matrix_ref, packed, sign, fresh):
        def step(t, carry):
            rows = pl.ds(t * row_tile, row_tile)
            value = product(matrix_ref, rows, packed)
            if fresh:
                accum[rows, :] = value
            else:
                accum[rows, :] = accum[rows, :] + sign * value
            return carry

        lax.fori_loop(0, row_tiles, step, 0)

    for k in range(STEPS):
        @pl.when(own_block == k)
        def _():
            resid[member] = pack(accum[:top, :], accum[top:, :]).astype(BF16)
            for d in range(1, group):
                resid_copy((member + d) % group).start()
            inv_own.wait()
            add_product(inv.at[member], resid[member], 1.0, True)
            for d in range(1, group):
                peer = (member + d) % group
                pltpu.make_async_copy(inv_hbm.at[pl.ds(0, own_rows)], inv.at[peer], inv_sem.at[peer]).wait()
                pltpu.make_async_copy(resid.at[peer], resid.at[peer], resid_recv.at[peer]).wait()
                add_product(inv.at[peer], resid[peer], 1.0, False)
            if k + 1 < STEPS:
                newest[k, member] = pack(accum[:top, :], accum[top:, :]).astype(BF16)
                for j in range(k + 1, STEPS):
                    new_copy(k, j).start()
            out_ref[...] = jnp.swapaxes(accum[:, :width], 0, 1).astype(BF16)

        if k + 1 < STEPS:
            @pl.when(own_block > k)
            def _():
                ref = newest.at[k, member]
                pltpu.make_async_copy(ref, ref, new_recv.at[k, member]).wait()
                for d in range(1, group):
                    forward_copy(k, (member + d) % group).start()
                for m in range(group):
                    band_copy(k, m).wait()
                add_product(band.at[k, member], newest[k, member], -1.0, False)
                for d in range(1, group):
                    peer = (member + d) % group
                    ref = newest.at[k, peer]
                    pltpu.make_async_copy(ref, ref, new_recv.at[k, peer]).wait()
                    add_product(band.at[k, peer], newest[k, peer], -1.0, False)

    def sent(which, up):
        for chunk in range(CHUNKS):
            for way in (True, False):
                if up is None or up == way:
                    @pl.when(s < n_slab - 1 if way else s > 0)
                    def _():
                        shard_copy(which, chunk, way, False).wait_send()
        pltpu.make_async_copy(arrived.at[which], arrived.at[which], part_send.at[which]).wait()

        @pl.when(jnp.logical_not(is_self(which)))
        def _():
            red_remote(which).wait_send()

    for t in range(n_slab):
        at_distance(t, sent)
    for d in range(1, group):
        peer = (member + d) % group
        inv_remote(peer).wait_send()
        resid_copy(peer).wait_send()
    for k in range(STEPS - 1):
        @pl.when(own_block == k)
        def _():
            for j in range(k + 1, STEPS):
                new_copy(k, j).wait_send()

        @pl.when(own_block > k)
        def _():
            for d in range(1, group):
                forward_copy(k, (member + d) % group).wait_send()


def body(n_blk, n_slab, old_factor, solved, band, inv_diag, rhs):
    window, depth = old_factor.shape
    own_rows, width = rhs.shape
    block_rows = inv_diag.shape[0]
    group = block_rows // own_rows
    half = window // n_blk // 2
    per_owner = own_rows // (2 * half)
    lanes = 2 * width
    tiles = 4
    dma = pltpu.SemaphoreType.DMA
    vmem = pl.BlockSpec(memory_space=pltpu.VMEM)
    hbm = pl.BlockSpec(memory_space=pl.ANY)
    return pl.pallas_call(
        functools.partial(kernel, n_blk, n_slab),
        out_shape=jax.ShapeDtypeStruct((width, own_rows), BF16),
        in_specs=[hbm, hbm, hbm, hbm, vmem],
        out_specs=vmem,
        scratch_shapes=[
            pltpu.VMEM((window, depth), BF16),
            pltpu.VMEM((STEPS - 1, group, own_rows, own_rows), BF16),
            pltpu.VMEM((group, own_rows, own_rows), BF16),
            pltpu.VMEM((n_slab, CHUNKS, width, depth // CHUNKS), BF16),
            pltpu.VMEM((depth // CHUNKS, width), BF16),
            pltpu.VMEM((2, window, width), F32),
            pltpu.VMEM((n_slab, n_blk, half, lanes), BF16),
            pltpu.VMEM((n_slab, n_blk - 1, half, lanes), BF16),
            pltpu.VMEM((n_slab, half, lanes), F32),
            pltpu.VMEM((per_owner, half, lanes), F32),
            pltpu.VMEM((own_rows, lanes), F32),
            pltpu.VMEM((group, own_rows // 2, lanes), BF16),
            pltpu.VMEM((STEPS - 1, group, own_rows // 2, lanes), BF16),
            dma((tiles,)),
            dma((STEPS - 1, group)),
            dma((group,)),
            dma((group,)),
            dma((n_slab, CHUNKS)),
            dma((n_slab, CHUNKS)),
            dma((n_slab, CHUNKS)),
            dma((n_slab,)),
            dma((n_slab,)),
            dma((n_slab,)),
            dma((per_owner,)),
            dma((group,)),
            dma((group,)),
            dma((STEPS - 1, STEPS)),
            dma((STEPS - 1, group)),
            dma((STEPS - 1, group)),
        ],
        compiler_params=pltpu.CompilerParams(has_side_effects=True, vmem_limit_bytes=60 * 1024 * 1024),
        name="forward_window",
    )(old_factor, solved.T, band, inv_diag, rhs.T).T


def solution(mesh):
    return jax.shard_map(
        functools.partial(body, mesh.shape["blk"], mesh.shape["slab"]),
        mesh=mesh,
        in_specs=(
            P("slab", "blk"),
            P("blk", "slab"),
            P("blk", None),
            P(None, "blk"),
            P("blk", "slab"),
        ),
        out_specs=P("blk", "slab"),
        check_vma=False,
    )
```

```python
import functools

import jax
import jax.numpy as jnp
from jax import lax
from jax.experimental import pallas as pl
from jax.experimental.pallas import tpu as pltpu
from jax.sharding import PartitionSpec as P

STEPS = 4
CHUNKS = 2
MESH = pl.DeviceIdType.MESH
F32 = jnp.float32
BF16 = jnp.bfloat16


def swap_halves(value):
    return pltpu.roll(value, value.shape[1] // 2, 1)


def left_half(shape):
    return lax.broadcasted_iota(jnp.int32, shape, 1) < shape[1] // 2


def pack(upper, lower):
    return jnp.where(left_half(upper.shape), upper, swap_halves(lower))


def product(matrix_ref, rows, packed):
    half = packed.shape[0]
    first = jnp.dot(matrix_ref[rows, :half], packed, preferred_element_type=F32)
    second = jnp.dot(matrix_ref[rows, half:], packed, preferred_element_type=F32)
    return first + swap_halves(second)


def kernel(
    n_blk,
    n_slab,
    factor_hbm,
    solved_hbm,
    band_hbm,
    inv_hbm,
    rhs_ref,
    out_ref,
    factor,
    band,
    inv,
    shards,
    columns,
    partial,
    parts,
    arrived,
    reduced,
    earlier,
    accum,
    resid,
    newest,
    factor_sem,
    band_sem,
    inv_sem,
    inv_send,
    shard_recv,
    up_send,
    down_send,
    part_send,
    part_recv,
    red_send,
    red_recv,
    resid_send,
    resid_recv,
    new_send,
    new_recv,
    fwd_send,
):
    b = lax.axis_index("blk")
    s = lax.axis_index("slab")
    width, own_rows = rhs_ref.shape
    block_rows = inv_hbm.shape[0]
    group = block_rows // own_rows
    own_block = b // group
    member = b % group
    window = factor_hbm.shape[0]
    piece = shards.shape[3]
    half = parts.shape[2]
    per_owner = own_rows // (2 * half)
    owners = window // own_rows
    tiles = factor_sem.shape[0]
    tile = window // tiles

    def remote(src, dst, send, recv, blk, slab):
        return pltpu.make_async_remote_copy(
            src_ref=src, dst_ref=dst, send_sem=send, recv_sem=recv,
            device_id=(blk, slab), device_id_type=MESH,
        )

    barrier = pltpu.get_barrier_semaphore()

    def greet(blk, slab):
        pl.semaphore_signal(barrier, inc=1, device_id=(blk, slab), device_id_type=MESH)

    @pl.when(s > 0)
    def _():
        greet(b, s - 1)

    @pl.when(s < n_slab - 1)
    def _():
        greet(b, s + 1)

    for d in range(1, n_blk):
        greet(lax.rem(b + d, n_blk), s)
    pl.semaphore_wait(barrier, n_blk - 1 + (s > 0).astype(jnp.int32) + (s < n_slab - 1).astype(jnp.int32))

    def shard_copy(which, chunk, up, own):
        ref = shards.at[which, chunk]
        source = solved_hbm.at[:, pl.ds(chunk * piece, piece)] if own else ref
        send = up_send if up else down_send
        return remote(source, ref, send.at[which, chunk], shard_recv.at[which, chunk], b, s + 1 if up else s - 1)

    def pass_on(which, chunk, up, own=False):
        @pl.when(s < n_slab - 1 if up else s > 0)
        def _():
            shard_copy(which, chunk, up, own).start()

    def own_copy(chunk):
        return pltpu.make_async_copy(
            solved_hbm.at[:, pl.ds(chunk * piece, piece)], shards.at[s, chunk], shard_recv.at[s, chunk]
        )

    for chunk in range(CHUNKS):
        pass_on(s, chunk, True, True)
        pass_on(s, chunk, False, True)
        own_copy(chunk).start()

    def factor_copy(t):
        rows = pl.ds(t * tile, tile)
        return pltpu.make_async_copy(factor_hbm.at[rows], factor.at[rows], factor_sem.at[t])

    for t in range(tiles):
        factor_copy(t).start()

    def inv_remote(peer):
        return remote(
            inv_hbm.at[pl.ds(peer * own_rows, own_rows)], inv.at[member],
            inv_send.at[peer], inv_sem.at[member], own_block * group + peer, s,
        )

    inv_own = pltpu.make_async_copy(
        inv_hbm.at[pl.ds(member * own_rows, own_rows)], inv.at[member], inv_sem.at[member]
    )
    inv_own.start()
    for d in range(1, group):
        inv_remote((member + d) % group).start()

    def band_copy(k, m):
        return pltpu.make_async_copy(
            band_hbm.at[:, pl.ds(k * block_rows + m * own_rows, own_rows)], band.at[k, m], band_sem.at[k, m]
        )

    for k in range(STEPS - 1):
        @pl.when(own_block > k)
        def _():
            for m in range(group):
                band_copy(k, m).start()

    def part_copy(which, c):
        return remote(
            parts.at[which, c], arrived.at[which, lax.rem(b - c + n_blk, n_blk) - 1],
            part_send.at[which], part_recv.at[which], c, s,
        )

    def multiply(which, chunk, first_time, side):
        columns[...] = jnp.swapaxes(shards[which, chunk].astype(F32), 0, 1).astype(BF16)
        span = slice(chunk * piece, (chunk + 1) * piece)
        per_tile = tile // (2 * half)

        def step(i, carry):
            t = lax.rem(i + lax.div(b * tiles, n_blk), tiles)
            if first_time and chunk == 0:
                factor_copy(t).wait()
            rows = pl.ds(t * tile, tile)
            value = jnp.dot(factor[rows, span], columns[...], preferred_element_type=F32)
            if chunk > 0:
                value = partial[side, rows, :] + value
            if chunk < CHUNKS - 1:
                partial[side, rows, :] = value
                return carry
            for i in range(per_tile):
                base = i * 2 * half
                c = t * per_tile + i
                packed = jnp.concatenate([value[base : base + half], value[base + half : base + 2 * half]], axis=1)
                parts[which, c] = packed.astype(BF16)

                @pl.when(c != b)
                def _():
                    part_copy(which, c).start()

            return carry

        lax.fori_loop(0, tiles, step, 0)

    def red_remote(which):
        return remote(
            reduced.at[which], earlier.at[b % per_owner],
            red_send.at[which], red_recv.at[b % per_owner], s * owners + b // per_owner, which,
        )

    def red_local(which):
        return pltpu.make_async_copy(reduced.at[which], earlier.at[b % per_owner], red_recv.at[b % per_owner])

    def is_self(which):
        return jnp.logical_and(which == s, b == s * owners + b // per_owner)

    def all_parts(which):
        return pltpu.make_async_copy(arrived.at[which], arrived.at[which], part_recv.at[which])

    def combine(which):
        all_parts(which).wait()
        total = parts[which, b].astype(F32)
        for d in range(n_blk - 1):
            total = total + arrived[which, d].astype(F32)
        reduced[which] = total

        @pl.when(is_self(which))
        def _():
            red_local(which).start()

        @pl.when(jnp.logical_not(is_self(which)))
        def _():
            red_remote(which).start()

    def take(which, chunk, up):
        ref = shards.at[which, chunk]
        remote(ref, ref, up_send.at[which, chunk], shard_recv.at[which, chunk], b, s).wait_recv()
        pass_on(which, chunk, up)

    def at_distance(t, action):
        if t == 0:
            action(s, None)
            return

        @pl.when(s >= t)
        def _():
            action(s - t, True)

        @pl.when(s + t < n_slab)
        def _():
            action(s + t, False)

    for chunk in range(CHUNKS):
        own_copy(chunk).wait()
        multiply(s, chunk, True, 0)
    for t in range(1, n_slab):
        for chunk in range(CHUNKS):
            at_distance(t, lambda which, up: take(which, chunk, up))
            at_distance(t, lambda which, up: multiply(which, chunk, False, 0 if up else 1))
        at_distance(t - 1, lambda which, up: combine(which))
    at_distance(n_slab - 1, lambda which, up: combine(which))

    accum[:, :width] = jnp.swapaxes(rhs_ref[...].astype(F32), 0, 1)
    for i in range(per_owner):
        pltpu.make_async_copy(reduced.at[0], earlier.at[i], red_recv.at[i]).wait()
        base = i * 2 * half
        value = earlier[i]
        accum[base : base + half, :width] = accum[base : base + half, :width] - value[:, :width]
        low = swap_halves(value)
        accum[base + half : base + 2 * half, :width] = accum[base + half : base + 2 * half, :width] - low[:, :width]

    top = own_rows // 2
    row_tiles = max(1, own_rows // 256)
    row_tile = own_rows // row_tiles

    def resid_copy(peer):
        ref = resid.at[member]
        return remote(ref, ref, resid_send.at[peer], resid_recv.at[member], own_block * group + peer, s)

    def new_copy(k, j):
        ref = newest.at[k, member]
        return remote(ref, ref, new_send.at[k, j], new_recv.at[k, member], j * group + member, s)

    def forward_copy(k, peer):
        ref = newest.at[k, member]
        return remote(ref, ref, fwd_send.at[k, peer], new_recv.at[k, member], own_block * group + peer, s)

    def add_product(matrix_ref, packed, sign, fresh):
        def step(t, carry):
            rows = pl.ds(t * row_tile, row_tile)
            value = product(matrix_ref, rows, packed)
            if fresh:
                accum[rows, :] = value
            else:
                accum[rows, :] = accum[rows, :] + sign * value
            return carry

        lax.fori_loop(0, row_tiles, step, 0)

    for k in range(STEPS):
        @pl.when(own_block == k)
        def _():
            resid[member] = pack(accum[:top, :], accum[top:, :]).astype(BF16)
            for d in range(1, group):
                resid_copy((member + d) % group).start()
            inv_own.wait()
            add_product(inv.at[member], resid[member], 1.0, True)
            for d in range(1, group):
                peer = (member + d) % group
                pltpu.make_async_copy(inv_hbm.at[pl.ds(0, own_rows)], inv.at[peer], inv_sem.at[peer]).wait()
                pltpu.make_async_copy(resid.at[peer], resid.at[peer], resid_recv.at[peer]).wait()
                add_product(inv.at[peer], resid[peer], 1.0, False)
            if k + 1 < STEPS:
                newest[k, member] = pack(accum[:top, :], accum[top:, :]).astype(BF16)
                for j in range(k + 1, STEPS):
                    new_copy(k, j).start()
            out_ref[...] = jnp.swapaxes(accum[:, :width], 0, 1).astype(BF16)

        if k + 1 < STEPS:
            @pl.when(own_block > k)
            def _():
                ref = newest.at[k, member]
                pltpu.make_async_copy(ref, ref, new_recv.at[k, member]).wait()
                for d in range(1, group):
                    forward_copy(k, (member + d) % group).start()
                for m in range(group):
                    band_copy(k, m).wait()
                add_product(band.at[k, member], newest[k, member], -1.0, False)
                for d in range(1, group):
                    peer = (member + d) % group
                    ref = newest.at[k, peer]
                    pltpu.make_async_copy(ref, ref, new_recv.at[k, peer]).wait()
                    add_product(band.at[k, peer], newest[k, peer], -1.0, False)

    def sent(which, up):
        for chunk in range(CHUNKS):
            for way in (True, False):
                if up is None or up == way:
                    @pl.when(s < n_slab - 1 if way else s > 0)
                    def _():
                        shard_copy(which, chunk, way, False).wait_send()
        pltpu.make_async_copy(arrived.at[which], arrived.at[which], part_send.at[which]).wait()

        @pl.when(jnp.logical_not(is_self(which)))
        def _():
            red_remote(which).wait_send()

    for t in range(n_slab):
        at_distance(t, sent)
    for d in range(1, group):
        peer = (member + d) % group
        inv_remote(peer).wait_send()
        resid_copy(peer).wait_send()
    for k in range(STEPS - 1):
        @pl.when(own_block == k)
        def _():
            for j in range(k + 1, STEPS):
                new_copy(k, j).wait_send()

        @pl.when(own_block > k)
        def _():
            for d in range(1, group):
                forward_copy(k, (member + d) % group).wait_send()


def body(n_blk, n_slab, old_factor, solved, band, inv_diag, rhs):
    window, depth = old_factor.shape
    own_rows, width = rhs.shape
    block_rows = inv_diag.shape[0]
    group = block_rows // own_rows
    half = window // n_blk // 2
    per_owner = own_rows // (2 * half)
    lanes = 2 * width
    tiles = 4
    dma = pltpu.SemaphoreType.DMA
    vmem = pl.BlockSpec(memory_space=pltpu.VMEM)
    hbm = pl.BlockSpec(memory_space=pl.ANY)
    return pl.pallas_call(
        functools.partial(kernel, n_blk, n_slab),
        out_shape=jax.ShapeDtypeStruct((width, own_rows), BF16),
        in_specs=[hbm, hbm, hbm, hbm, vmem],
        out_specs=vmem,
        scratch_shapes=[
            pltpu.VMEM((window, depth), BF16),
            pltpu.VMEM((STEPS - 1, group, own_rows, own_rows), BF16),
            pltpu.VMEM((group, own_rows, own_rows), BF16),
            pltpu.VMEM((n_slab, CHUNKS, width, depth // CHUNKS), BF16),
            pltpu.VMEM((depth // CHUNKS, width), BF16),
            pltpu.VMEM((2, window, width), F32),
            pltpu.VMEM((n_slab, n_blk, half, lanes), BF16),
            pltpu.VMEM((n_slab, n_blk - 1, half, lanes), BF16),
            pltpu.VMEM((n_slab, half, lanes), F32),
            pltpu.VMEM((per_owner, half, lanes), F32),
            pltpu.VMEM((own_rows, lanes), F32),
            pltpu.VMEM((group, own_rows // 2, lanes), BF16),
            pltpu.VMEM((STEPS - 1, group, own_rows // 2, lanes), BF16),
            dma((tiles,)),
            dma((STEPS - 1, group)),
            dma((group,)),
            dma((group,)),
            dma((n_slab, CHUNKS)),
            dma((n_slab, CHUNKS)),
            dma((n_slab, CHUNKS)),
            dma((n_slab,)),
            dma((n_slab,)),
            dma((n_slab,)),
            dma((per_owner,)),
            dma((group,)),
            dma((group,)),
            dma((STEPS - 1, STEPS)),
            dma((STEPS - 1, group)),
            dma((STEPS - 1, group)),
        ],
        compiler_params=pltpu.CompilerParams(collective_id=0, has_side_effects=True, vmem_limit_bytes=60 * 1024 * 1024),
        name="forward_window",
    )(old_factor, solved.T, band, inv_diag, rhs.T).T


def solution(mesh):
    return jax.shard_map(
        functools.partial(body, mesh.shape["blk"], mesh.shape["slab"]),
        mesh=mesh,
        in_specs=(
            P("slab", "blk"),
            P("blk", "slab"),
            P("blk", None),
            P(None, "blk"),
            P("blk", "slab"),
        ),
        out_specs=P("blk", "slab"),
        check_vma=False,
    )
```

```python
import functools

import jax
import jax.numpy as jnp
from jax import lax
from jax.experimental import pallas as pl
from jax.experimental.pallas import tpu as pltpu
from jax.sharding import PartitionSpec as P

STEPS = 4
CHUNKS = 2
MESH = pl.DeviceIdType.MESH
F32 = jnp.float32
BF16 = jnp.bfloat16


def swap_halves(value):
    return pltpu.roll(value, value.shape[1] // 2, 1)


def left_half(shape):
    return lax.broadcasted_iota(jnp.int32, shape, 1) < shape[1] // 2


def pack(upper, lower):
    return jnp.where(left_half(upper.shape), upper, swap_halves(lower))


def product(matrix_ref, rows, packed, start, half):
    count = packed.shape[0]
    upper = matrix_ref[rows, start : start + count]
    lower = matrix_ref[rows, half + start : half + start + count]
    first = jnp.dot(upper, packed, preferred_element_type=F32)
    second = jnp.dot(lower, packed, preferred_element_type=F32)
    return first + swap_halves(second)


def kernel(
    n_blk,
    n_slab,
    factor_hbm,
    solved_hbm,
    band_hbm,
    inv_hbm,
    rhs_ref,
    out_ref,
    factor,
    band,
    inv,
    shards,
    columns,
    partial,
    parts,
    arrived,
    reduced,
    earlier,
    accum,
    resid,
    newest,
    factor_sem,
    band_sem,
    inv_sem,
    inv_send,
    shard_recv,
    up_send,
    down_send,
    part_send,
    part_recv,
    red_send,
    red_recv,
    resid_send,
    resid_recv,
    new_send,
    new_recv,
    fwd_send,
):
    b = lax.axis_index("blk")
    s = lax.axis_index("slab")
    width, own_rows = rhs_ref.shape
    block_rows = inv_hbm.shape[0]
    group = block_rows // own_rows
    own_block = b // group
    member = b % group
    window = factor_hbm.shape[0]
    piece = shards.shape[3]
    half = parts.shape[2]
    per_owner = own_rows // (2 * half)
    owners = window // own_rows
    tiles = factor_sem.shape[0]
    tile = window // tiles

    def remote(src, dst, send, recv, blk, slab):
        return pltpu.make_async_remote_copy(
            src_ref=src, dst_ref=dst, send_sem=send, recv_sem=recv,
            device_id=(blk, slab), device_id_type=MESH,
        )

    barrier = pltpu.get_barrier_semaphore()

    def greet(blk, slab):
        pl.semaphore_signal(barrier, inc=1, device_id=(blk, slab), device_id_type=MESH)

    @pl.when(s > 0)
    def _():
        greet(b, s - 1)

    @pl.when(s < n_slab - 1)
    def _():
        greet(b, s + 1)

    for d in range(1, n_blk):
        greet(lax.rem(b + d, n_blk), s)
    pl.semaphore_wait(barrier, n_blk - 1 + (s > 0).astype(jnp.int32) + (s < n_slab - 1).astype(jnp.int32))

    def shard_copy(which, chunk, up, own):
        ref = shards.at[which, chunk]
        source = solved_hbm.at[:, pl.ds(chunk * piece, piece)] if own else ref
        send = up_send if up else down_send
        return remote(source, ref, send.at[which, chunk], shard_recv.at[which, chunk], b, s + 1 if up else s - 1)

    def pass_on(which, chunk, up, own=False):
        @pl.when(s < n_slab - 1 if up else s > 0)
        def _():
            shard_copy(which, chunk, up, own).start()

    def own_copy(chunk):
        return pltpu.make_async_copy(
            solved_hbm.at[:, pl.ds(chunk * piece, piece)], shards.at[s, chunk], shard_recv.at[s, chunk]
        )

    for chunk in range(CHUNKS):
        pass_on(s, chunk, True, True)
        pass_on(s, chunk, False, True)
        own_copy(chunk).start()

    def factor_copy(t):
        rows = pl.ds(t * tile, tile)
        return pltpu.make_async_copy(factor_hbm.at[rows], factor.at[rows], factor_sem.at[t])

    for t in range(tiles):
        factor_copy(t).start()

    def inv_remote(peer):
        return remote(
            inv_hbm.at[pl.ds(peer * own_rows, own_rows)], inv.at[member],
            inv_send.at[peer], inv_sem.at[member], own_block * group + peer, s,
        )

    inv_own = pltpu.make_async_copy(
        inv_hbm.at[pl.ds(member * own_rows, own_rows)], inv.at[member], inv_sem.at[member]
    )
    inv_own.start()
    for d in range(1, group):
        inv_remote((member + d) % group).start()

    def band_copy(k, m):
        return pltpu.make_async_copy(
            band_hbm.at[:, pl.ds(k * block_rows + m * own_rows, own_rows)], band.at[k, m], band_sem.at[k, m]
        )

    for k in range(STEPS - 1):
        @pl.when(own_block > k)
        def _():
            for m in range(group):
                band_copy(k, m).start()

    def part_copy(which, c):
        return remote(
            parts.at[which, c], arrived.at[which, lax.rem(b - c + n_blk, n_blk) - 1],
            part_send.at[which], part_recv.at[which], c, s,
        )

    def multiply(which, chunk, first_time, side):
        columns[...] = jnp.swapaxes(shards[which, chunk].astype(F32), 0, 1).astype(BF16)
        span = slice(chunk * piece, (chunk + 1) * piece)
        per_tile = tile // (2 * half)

        def step(i, carry):
            t = lax.rem(i + lax.div(b * tiles, n_blk), tiles)
            if first_time and chunk == 0:
                factor_copy(t).wait()
            rows = pl.ds(t * tile, tile)
            value = jnp.dot(factor[rows, span], columns[...], preferred_element_type=F32)
            if chunk > 0:
                value = partial[side, rows, :] + value
            if chunk < CHUNKS - 1:
                partial[side, rows, :] = value
                return carry
            for i in range(per_tile):
                base = i * 2 * half
                c = t * per_tile + i
                packed = jnp.concatenate([value[base : base + half], value[base + half : base + 2 * half]], axis=1)
                parts[which, c] = packed.astype(BF16)

                @pl.when(c != b)
                def _():
                    part_copy(which, c).start()

            return carry

        lax.fori_loop(0, tiles, step, 0)

    def red_remote(which):
        return remote(
            reduced.at[which], earlier.at[b % per_owner],
            red_send.at[which], red_recv.at[b % per_owner], s * owners + b // per_owner, which,
        )

    def red_local(which):
        return pltpu.make_async_copy(reduced.at[which], earlier.at[b % per_owner], red_recv.at[b % per_owner])

    def is_self(which):
        return jnp.logical_and(which == s, b == s * owners + b // per_owner)

    def all_parts(which):
        return pltpu.make_async_copy(arrived.at[which], arrived.at[which], part_recv.at[which])

    def combine(which):
        all_parts(which).wait()
        total = parts[which, b].astype(F32)
        for d in range(n_blk - 1):
            total = total + arrived[which, d].astype(F32)
        reduced[which] = total

        @pl.when(is_self(which))
        def _():
            red_local(which).start()

        @pl.when(jnp.logical_not(is_self(which)))
        def _():
            red_remote(which).start()

    def take(which, chunk, up):
        ref = shards.at[which, chunk]
        remote(ref, ref, up_send.at[which, chunk], shard_recv.at[which, chunk], b, s).wait_recv()
        pass_on(which, chunk, up)

    def at_distance(t, action):
        if t == 0:
            action(s, None)
            return

        @pl.when(s >= t)
        def _():
            action(s - t, True)

        @pl.when(s + t < n_slab)
        def _():
            action(s + t, False)

    for chunk in range(CHUNKS):
        own_copy(chunk).wait()
        multiply(s, chunk, True, 0)
    for t in range(1, n_slab):
        for chunk in range(CHUNKS):
            at_distance(t, lambda which, up: take(which, chunk, up))
            at_distance(t, lambda which, up: multiply(which, chunk, False, 0 if up else 1))
        at_distance(t - 1, lambda which, up: combine(which))
    at_distance(n_slab - 1, lambda which, up: combine(which))

    accum[:, :width] = jnp.swapaxes(rhs_ref[...].astype(F32), 0, 1)
    for i in range(per_owner):
        pltpu.make_async_copy(reduced.at[0], earlier.at[i], red_recv.at[i]).wait()
        base = i * 2 * half
        value = earlier[i]
        accum[base : base + half, :width] = accum[base : base + half, :width] - value[:, :width]
        low = swap_halves(value)
        accum[base + half : base + 2 * half, :width] = accum[base + half : base + 2 * half, :width] - low[:, :width]

    top = own_rows // 2
    cuts = newest.shape[2]
    cut = newest.shape[3]
    row_tile = min(own_rows, 512)
    row_tiles = own_rows // row_tile

    def resid_copy(peer):
        ref = resid.at[member]
        return remote(ref, ref, resid_send.at[peer], resid_recv.at[member], own_block * group + peer, s)

    def new_copy(k, j, i):
        ref = newest.at[k, member, i]
        return remote(ref, ref, new_send.at[k, j, i], new_recv.at[k, member, i], j * group + member, s)

    def forward_copy(k, peer, i):
        ref = newest.at[k, member, i]
        return remote(ref, ref, fwd_send.at[k, peer, i], new_recv.at[k, member, i], own_block * group + peer, s)

    def await_new(k, m, i):
        ref = newest.at[k, m, i]
        pltpu.make_async_copy(ref, ref, new_recv.at[k, m, i]).wait()

    def add_product(matrix_ref, packed, start, sign, fresh):
        def step(t, carry):
            rows = pl.ds(t * row_tile, row_tile)
            value = product(matrix_ref, rows, packed, start, top)
            if fresh:
                accum[rows, :] = value
            else:
                accum[rows, :] = accum[rows, :] + sign * value
            return carry

        lax.fori_loop(0, row_tiles, step, 0)

    for k in range(STEPS):
        @pl.when(own_block == k)
        def _():
            resid[member] = pack(accum[:top, :], accum[top:, :]).astype(BF16)
            for d in range(1, group):
                resid_copy((member + d) % group).start()
            inv_own.wait()
            add_product(inv.at[member], resid[member], 0, 1.0, True)
            for d in range(1, group):
                peer = (member + d) % group
                pltpu.make_async_copy(inv_hbm.at[pl.ds(0, own_rows)], inv.at[peer], inv_sem.at[peer]).wait()
                pltpu.make_async_copy(resid.at[peer], resid.at[peer], resid_recv.at[peer]).wait()
                if d < group - 1:
                    add_product(inv.at[peer], resid[peer], 0, 1.0, False)
            last = (member + group - 1) % group
            for i in range(cuts):
                upper = slice(i * cut, (i + 1) * cut)
                lower = slice(top + i * cut, top + (i + 1) * cut)
                for rows in (upper, lower):
                    accum[rows, :] = accum[rows, :] + product(inv.at[last], rows, resid[last], 0, top)
                if k + 1 < STEPS:
                    newest[k, member, i] = pack(accum[upper, :], accum[lower, :]).astype(BF16)
                    for j in range(k + 1, STEPS):
                        new_copy(k, j, i).start()
            out_ref[...] = jnp.swapaxes(accum[:, :width], 0, 1).astype(BF16)

        if k + 1 < STEPS:
            @pl.when(own_block > k)
            def _():
                for i in range(cuts):
                    await_new(k, member, i)
                    for d in range(1, group):
                        forward_copy(k, (member + d) % group, i).start()
                    if i == 0:
                        for m in range(group):
                            band_copy(k, m).wait()
                    add_product(band.at[k, member], newest[k, member, i], i * cut, -1.0, False)
                for d in range(1, group):
                    peer = (member + d) % group
                    for i in range(cuts):
                        await_new(k, peer, i)
                        add_product(band.at[k, peer], newest[k, peer, i], i * cut, -1.0, False)

    def sent(which, up):
        for chunk in range(CHUNKS):
            for way in (True, False):
                if up is None or up == way:
                    @pl.when(s < n_slab - 1 if way else s > 0)
                    def _():
                        shard_copy(which, chunk, way, False).wait_send()
        pltpu.make_async_copy(arrived.at[which], arrived.at[which], part_send.at[which]).wait()

        @pl.when(jnp.logical_not(is_self(which)))
        def _():
            red_remote(which).wait_send()

    for t in range(n_slab):
        at_distance(t, sent)
    for d in range(1, group):
        peer = (member + d) % group
        inv_remote(peer).wait_send()
        resid_copy(peer).wait_send()
    for k in range(STEPS - 1):
        @pl.when(own_block == k)
        def _():
            for j in range(k + 1, STEPS):
                for i in range(cuts):
                    new_copy(k, j, i).wait_send()

        @pl.when(own_block > k)
        def _():
            for d in range(1, group):
                for i in range(cuts):
                    forward_copy(k, (member + d) % group, i).wait_send()


def body(n_blk, n_slab, old_factor, solved, band, inv_diag, rhs):
    window, depth = old_factor.shape
    own_rows, width = rhs.shape
    block_rows = inv_diag.shape[0]
    group = block_rows // own_rows
    half = window // n_blk // 2
    per_owner = own_rows // (2 * half)
    lanes = 2 * width
    tiles = 4
    cuts = 2 if own_rows >= 512 else 1
    dma = pltpu.SemaphoreType.DMA
    vmem = pl.BlockSpec(memory_space=pltpu.VMEM)
    hbm = pl.BlockSpec(memory_space=pl.ANY)
    return pl.pallas_call(
        functools.partial(kernel, n_blk, n_slab),
        out_shape=jax.ShapeDtypeStruct((width, own_rows), BF16),
        in_specs=[hbm, hbm, hbm, hbm, vmem],
        out_specs=vmem,
        scratch_shapes=[
            pltpu.VMEM((window, depth), BF16),
            pltpu.VMEM((STEPS - 1, group, own_rows, own_rows), BF16),
            pltpu.VMEM((group, own_rows, own_rows), BF16),
            pltpu.VMEM((n_slab, CHUNKS, width, depth // CHUNKS), BF16),
            pltpu.VMEM((depth // CHUNKS, width), BF16),
            pltpu.VMEM((2, window, width), F32),
            pltpu.VMEM((n_slab, n_blk, half, lanes), BF16),
            pltpu.VMEM((n_slab, n_blk - 1, half, lanes), BF16),
            pltpu.VMEM((n_slab, half, lanes), F32),
            pltpu.VMEM((per_owner, half, lanes), F32),
            pltpu.VMEM((own_rows, lanes), F32),
            pltpu.VMEM((group, own_rows // 2, lanes), BF16),
            pltpu.VMEM((STEPS - 1, group, cuts, own_rows // 2 // cuts, lanes), BF16),
            dma((tiles,)),
            dma((STEPS - 1, group)),
            dma((group,)),
            dma((group,)),
            dma((n_slab, CHUNKS)),
            dma((n_slab, CHUNKS)),
            dma((n_slab, CHUNKS)),
            dma((n_slab,)),
            dma((n_slab,)),
            dma((n_slab,)),
            dma((per_owner,)),
            dma((group,)),
            dma((group,)),
            dma((STEPS - 1, STEPS, cuts)),
            dma((STEPS - 1, group, cuts)),
            dma((STEPS - 1, group, cuts)),
        ],
        compiler_params=pltpu.CompilerParams(collective_id=0, has_side_effects=True, vmem_limit_bytes=60 * 1024 * 1024),
        name="forward_window",
    )(old_factor, solved.T, band, inv_diag, rhs.T).T


def solution(mesh):
    return jax.shard_map(
        functools.partial(body, mesh.shape["blk"], mesh.shape["slab"]),
        mesh=mesh,
        in_specs=(
            P("slab", "blk"),
            P("blk", "slab"),
            P("blk", None),
            P(None, "blk"),
            P("blk", "slab"),
        ),
        out_specs=P("blk", "slab"),
        check_vma=False,
    )
```
